32 devices in a mesh: text: 4 (over z), det: 8 (over y, x, core).
Axes of the slice: x: 2, y: 2, z: 4, core: 2. Of those that a mesh axis runs over, the one named last changes fastest.
Arguments:
- prompt_embeds: bfloat16 [64, 16, 2048], P('text'), may hold values from -6 to 6
- prompt_len: int32 [64], P('text'), may hold values from 1 to 16
- norm_gain: float32 [2048], replicated, may hold values from 0.5 to 1.5
- w_up: bfloat16 [2048, 8192], P(None, 'det'), may hold values from -0.125 to 0.125
- w_down: bfloat16 [8192, 2048], P('det'), may hold values from -0.0625 to 0.0625
- final_gain: float32 [2048], replicated, may hold values from 0.25 to 1.75
- w_proj: bfloat16 [2048, 256], P('det'), may hold values from -0.125 to 0.125
- queries: bfloat16 [32, 1100, 256], P(('text', 'det')), may hold values from -6 to 6
- assign: int32 [32, 1100], P(('text', 'det')), may hold values from 0 to 127
- valid: int32 [32, 64], P(('text', 'det')), may hold values 0 or 1
Outputs:
- grad_up: float32 [2048, 8192], P('text', 'det')
- grad_down: float32 [8192, 2048], P('det', 'text')
- grad_proj: float32 [2048, 256], P('det')
- grad_queries: float32 [32, 1100, 256], P(('text', 'det'))
The draws below stay inside these ranges and needn't reach their ends.
Inputs may be any that keep to these rules, and one draw needn't show every extreme that they name: `prompt_len`: every prompt uses at least its first token. `assign`: A value of 64 or more means the query has no concept.
All inputs are finite; a program needn't handle non-finite values. No bound on the sum of `valid` on one device may be relied on, other than what follows from the above.
Results may differ from the reference program's by a relative error of at most 0.025.
Values may be sent and summed in bfloat16 or wider, within the bound.
No kernel may reach another device: no remote copies, remote signals or barrier semaphores. Data moves between devices by JAX's collectives and lax.ppermute only.
A program may use at most 64 MiB of HBM per device.

```python
import jax
import jax.numpy as jnp
from jax import lax

D = 2048
HID = 8192
DQ = 256
PROMPT = 16
QUERIES = 1100
CON_DEV = 16
CONCEPTS = 64
IMAGES = 32
N_TEXT = 4


def place_ends(array, own_key, low, largest):
    longest = array.shape.index(max(array.shape))
    spots = []
    for shift in (0, 1):
        where = [jax.random.randint(jax.random.fold_in(own_key, axis), (), 0, length) for axis, length in enumerate(array.shape)]
        where[longest] = (where[longest] + shift) % array.shape[longest]
        spots.append(tuple(where))
    return array.at[spots[0]].set(low).at[spots[1]].set(largest)


def block_levels(rng, dims, shards, low, largest):
    def one(dim, blocks):
        draws = jax.random.uniform(jax.random.fold_in(jax.random.fold_in(rng, 6), dim), (blocks,), jnp.float32, low / len(shards), largest / len(shards))
        return jnp.repeat(jnp.exp(draws), dims[dim] // blocks).reshape((-1,) + (1,) * (len(dims) - dim - 1))

    gain = one(*shards[0])
    for cut in shards[1:]:
        gain = gain * one(*cut)
    return gain


def normal_values(key, extent, width, limit, shards=(), dtype=jnp.bfloat16):
    entries = jax.random.normal(key, extent, jnp.float32) * width
    if len(shards) > 0:
        entries = block_levels(key, extent, shards, -0.22, 0.18) * entries
    return jnp.clip(entries, min=-limit, max=limit).astype(dtype)


def setup_inputs(seed: int = 0) -> dict:
    splits = jax.random.split(jax.random.key(seed), 11)
    prompt_embeds = normal_values(splits[0], (CONCEPTS, PROMPT, D), 1.0, 6.0, ((0, 4),))
    prompt_len = place_ends(jax.random.randint(splits[1], (CONCEPTS,), 1, PROMPT + 1), jax.random.fold_in(splits[1], 1), 1, PROMPT).astype(jnp.int32)
    norm_gain = jnp.clip(1.0 + 0.1 * jax.random.normal(splits[2], (D,), jnp.float32), 0.5, 1.5)
    w_up = normal_values(splits[3], (D, HID), D ** -0.5, 0.125, ((1, 8),))
    w_down = normal_values(splits[4], (HID, D), HID ** -0.5, 0.0625, ((0, 8),))
    final_gain = jnp.clip(1.0 + 0.15 * jax.random.normal(splits[5], (D,), jnp.float32), 0.25, 1.75)
    w_proj = normal_values(splits[6], (D, DQ), D ** -0.5, 0.125, ((0, 8),))
    queries = normal_values(splits[7], (IMAGES, QUERIES, DQ), 1.0, 6.0, ((0, 32),))
    assign = place_ends(jax.random.randint(splits[8], (IMAGES, QUERIES), 0, 2 * CONCEPTS), jax.random.fold_in(splits[8], 1), 0, (2 * CONCEPTS) - 1).astype(jnp.int32)
    valid = place_ends((jax.random.randint(splits[9], (IMAGES, CONCEPTS), 0, 16) < 1).astype(jnp.int32), jax.random.fold_in(splits[9], 1), 0, 1)
    return dict(prompt_embeds=prompt_embeds, prompt_len=prompt_len, norm_gain=norm_gain, w_up=w_up, w_down=w_down, final_gain=final_gain, w_proj=w_proj, queries=queries, assign=assign, valid=valid)


EPS = 1e-05
ALPHA = 0.25
LOGIT_BIAS = -2.0

def gelu_fn(values):
    return jax.nn.gelu(values, approximate=True)

def focal_total(scores, target, weight):
    log_pos = jax.nn.log_sigmoid(scores)
    log_neg = jax.nn.log_sigmoid(-scores)
    probab = jax.nn.sigmoid(scores)
    pos_term = -ALPHA * target * (1.0 - probab) ** 2 * log_pos
    neg_term = -(1.0 - ALPHA) * (1.0 - target) * probab ** 2 * log_neg
    return jnp.sum(weight * (pos_term + neg_term))

def norm_parts(values):
    row_mean = lax.optimization_barrier(jnp.mean(values, axis=-1, keepdims=True))
    centred = values - row_mean
    variance = lax.optimization_barrier(jnp.mean(centred * centred, axis=-1, keepdims=True))
    inv_scale = lax.rsqrt(variance + EPS)
    return (centred * inv_scale, inv_scale)

def reference(prompt_embeds, prompt_len, norm_gain, w_up, w_down, final_gain, w_proj, queries, assign, valid):
    tok_rows = CONCEPTS * PROMPT
    tokens = prompt_embeds.reshape(tok_rows, D).astype(jnp.float32)
    in_hat, _ = norm_parts(tokens)
    normed = (in_hat * norm_gain).astype(jnp.bfloat16)
    pre_act = jnp.dot(normed, w_up, preferred_element_type=jnp.float32)
    hidden_act, act_back = jax.vjp(gelu_fn, pre_act)
    hidden = hidden_act.astype(jnp.bfloat16)
    layer_out = tokens + jnp.dot(hidden, w_down, preferred_element_type=jnp.float32)
    out_hat, inv_scale = norm_parts(layer_out)
    final = out_hat * final_gain
    position = lax.broadcasted_iota(jnp.int32, (CONCEPTS, PROMPT), 1)
    lengths = prompt_len.astype(jnp.float32)
    pool_weight = (position < prompt_len[:, None]).astype(jnp.float32) / lengths[:, None]
    pooled = lax.optimization_barrier(jnp.sum(final.reshape(CONCEPTS, PROMPT, D) * pool_weight[:, :, None], axis=1))
    pooled_low = pooled.astype(jnp.bfloat16)
    concept_feat = jnp.dot(pooled_low, w_proj, preferred_element_type=jnp.float32).astype(jnp.bfloat16)
    score_scale = DQ ** (-0.5)

    def per_image(summed, item_parts):
        query_rows, chosen, allowed = item_parts
        scores = jnp.dot(query_rows, concept_feat.T, preferred_element_type=jnp.float32) * score_scale + LOGIT_BIAS
        column = lax.broadcasted_iota(jnp.int32, (QUERIES, CONCEPTS), 1)
        target = (chosen[:, None] == column).astype(jnp.float32)
        weight = jnp.broadcast_to(allowed[None, :].astype(jnp.float32), (QUERIES, CONCEPTS))
        score_grad = jax.grad(focal_total)(scores, target, weight).astype(jnp.bfloat16)
        query_grad = jnp.dot(score_grad, concept_feat, preferred_element_type=jnp.float32) * score_scale
        terms = jnp.dot(score_grad.T, query_rows, preferred_element_type=jnp.float32)
        return (summed + terms, query_grad)
    summed, grad_queries = lax.scan(per_image, jnp.zeros((CONCEPTS, DQ), jnp.float32), (queries, assign, valid))
    feat_grad = summed * (score_scale / IMAGES)
    grad_proj = jnp.dot(pooled_low.astype(jnp.float32).T, feat_grad, precision=lax.Precision.HIGHEST)
    pooled_grad = jnp.dot(feat_grad, w_proj.astype(jnp.float32).T, precision=lax.Precision.HIGHEST)
    final_grad = (pooled_grad[:, None, :] * pool_weight[:, :, None]).reshape(tok_rows, D)
    hat_grad = final_grad * final_gain
    mean_first = lax.optimization_barrier(jnp.mean(hat_grad, axis=-1, keepdims=True))
    mean_second = lax.optimization_barrier(jnp.mean(hat_grad * out_hat, axis=-1, keepdims=True))
    out_grad = ((hat_grad - mean_first - out_hat * mean_second) * inv_scale).astype(jnp.bfloat16)
    hidden_grad = jnp.dot(out_grad, w_down.T, preferred_element_type=jnp.float32)
    pre_grad = act_back(hidden_grad)[0].astype(jnp.bfloat16)
    group_rows = CON_DEV * PROMPT

    def group_sum(carry, item_parts):
        down_sum, up_sum = carry
        hidden_part, out_part, normed_part, pre_part = item_parts
        down_part = jnp.dot(hidden_part.T, out_part, preferred_element_type=jnp.float32)
        up_part = jnp.dot(normed_part.T, pre_part, preferred_element_type=jnp.float32)
        down_round = lax.optimization_barrier(down_part.astype(jnp.bfloat16)).astype(jnp.float32)
        up_round = lax.optimization_barrier(up_part.astype(jnp.bfloat16)).astype(jnp.float32)
        return ((down_sum + down_round, up_sum + up_round), None)
    start = (jnp.zeros((HID, D), jnp.float32), jnp.zeros((D, HID), jnp.float32))
    pieces = (hidden.reshape(N_TEXT, group_rows, HID), out_grad.reshape(N_TEXT, group_rows, D), normed.reshape(N_TEXT, group_rows, D), pre_grad.reshape(N_TEXT, group_rows, HID))
    (grad_down, grad_up), _ = lax.scan(group_sum, start, pieces)
    return (grad_up, grad_down, grad_proj, grad_queries)
```

```python
import jax
import jax.numpy as jnp
from jax import lax
from jax.sharding import PartitionSpec as P

EPS = 1e-05
ALPHA = 0.25
LOGIT_BIAS = -2.0
PACK = 128
ROOM = 24 << 20
LOW = jnp.bfloat16
FULL = jnp.float32


def gelu_fn(values):
    return jax.nn.gelu(values, approximate=True)


def gelu_both(values):
    act, slope = jax.jvp(gelu_fn, (values,), (jnp.ones_like(values),))
    return act.astype(LOW), slope.astype(LOW)


def focal_total(scores, target, weight):
    log_pos = jax.nn.log_sigmoid(scores)
    log_neg = jax.nn.log_sigmoid(-scores)
    probab = jax.nn.sigmoid(scores)
    pos_term = -ALPHA * target * (1.0 - probab) ** 2 * log_pos
    neg_term = -(1.0 - ALPHA) * (1.0 - target) * probab**2 * log_neg
    return jnp.sum(weight * (pos_term + neg_term))


def swap(values, axis, mask):
    size = lax.axis_size(axis)
    return lax.ppermute(values, axis, [(i, i ^ mask) for i in range(size)])


def bit_groups(size):
    bits = size.bit_length() - 1
    assert size == 1 << bits
    groups = [[0, 1]] if bits else []
    bit = 1
    while bit < bits:
        wide = min(2, bits - bit)
        groups.append([k << bit for k in range(1 << wide)])
        bit += wide
    return groups


def gather_det(values):
    offsets = [0]
    blocks = values[None]
    groups = bit_groups(lax.axis_size("det"))
    for masks in groups[1:] + groups[:1]:
        blocks = jnp.concatenate([blocks] + [swap(blocks, "det", m) for m in masks[1:]], 0)
        offsets = [m ^ o for m in masks for o in offsets]
    return blocks, offsets


def sum_det(values):
    for masks in bit_groups(lax.axis_size("det")):
        total = values.astype(FULL)
        for m in masks[1:]:
            total = total + swap(values, "det", m).astype(FULL)
        values = total.astype(LOW)
    return total


def scatter_det(values, index):
    for masks in bit_groups(lax.axis_size("det")):
        wide = len(masks)
        here = lax.rem(index, wide)
        index = lax.div(index, wide)
        split = values.reshape((values.shape[0] // wide, wide) + values.shape[1:])
        total = lax.dynamic_index_in_dim(split, here, 1, keepdims=False).astype(FULL)
        for n, m in enumerate(masks[1:], 1):
            away = lax.dynamic_index_in_dim(split, here ^ n, 1, keepdims=False)
            total = total + swap(away, "det", m).astype(FULL)
        values = total.astype(LOW)
    return total[0]


def dot_t(left, right):
    return lax.dot_general(left, right, (((1,), (1,)), ((), ())), preferred_element_type=FULL)


def dot_c(left, right):
    return lax.dot_general(left, right, (((0,), (0,)), ((), ())), preferred_element_type=FULL)


def dot_n(left, right):
    return jnp.dot(left, right, preferred_element_type=FULL)


def body_scatter(
    prompt_embeds, prompt_len, norm_gain, w_up, w_down, final_gain, w_proj, queries, assign, valid
):
    per_group, prompt, model_width = prompt_embeds.shape
    tok_rows = per_group * prompt
    det_size = lax.axis_size("det")
    share = model_width // det_size
    offset = lax.axis_index("det") * share
    tokens = prompt_embeds.reshape(tok_rows, model_width).astype(jnp.float32)
    row_mean = jnp.mean(tokens, axis=1, keepdims=True)
    centred = tokens - row_mean
    variance = jnp.mean(centred * centred, axis=1, keepdims=True)
    normed = (centred * lax.rsqrt(variance + EPS) * norm_gain).astype(jnp.bfloat16)
    pre_act = jnp.dot(normed, w_up, preferred_element_type=jnp.float32)
    hidden_act, act_back = jax.vjp(gelu_fn, pre_act)
    hidden = hidden_act.astype(jnp.bfloat16)
    partial_out = jnp.dot(hidden, w_down, preferred_element_type=jnp.float32)
    position = lax.broadcasted_iota(jnp.int32, (per_group, prompt), 1)
    lengths = prompt_len.astype(jnp.float32)
    pool_weight = (position < prompt_len[:, None]).astype(jnp.float32) / lengths[:, None]
    layer_out = tokens + lax.psum(partial_out.astype(jnp.bfloat16), "det").astype(jnp.float32)
    out_mean = jnp.mean(layer_out, axis=1, keepdims=True)
    out_centred = layer_out - out_mean
    out_var = jnp.mean(out_centred * out_centred, axis=1, keepdims=True)
    inv_scale = lax.rsqrt(out_var + EPS)
    out_hat = out_centred * inv_scale
    final = out_hat * final_gain
    pooled_full = jnp.sum(
        final.reshape(per_group, prompt, model_width) * pool_weight[:, :, None], axis=1
    )
    pooled_share = lax.dynamic_slice_in_dim(pooled_full, offset, share, 1)
    pooled_low = pooled_share.astype(jnp.bfloat16)
    feat_part = jnp.dot(pooled_low, w_proj, preferred_element_type=jnp.float32)
    concept_feat = lax.psum(feat_part, "det").astype(jnp.bfloat16)
    all_feat = lax.all_gather(concept_feat, "text", axis=0, tiled=True)
    concept_count = all_feat.shape[0]
    img_count, query_count, query_width = queries.shape
    query_rows = img_count * query_count
    flat_queries = queries.reshape(query_rows, query_width)
    score_scale = query_width ** (-0.5)
    scores = (
        lax.dot_general(
            flat_queries, all_feat, (((1,), (1,)), ((), ())), preferred_element_type=jnp.float32
        )
        * score_scale
        + LOGIT_BIAS
    )
    column = lax.broadcasted_iota(jnp.int32, (img_count, query_count, concept_count), 2)
    target = (assign[:, :, None] == column).astype(jnp.float32).reshape(query_rows, concept_count)
    weight = jnp.broadcast_to(
        valid[:, None, :].astype(jnp.float32), (img_count, query_count, concept_count)
    ).reshape(query_rows, concept_count)
    score_grad = jax.grad(focal_total)(scores, target, weight).astype(jnp.bfloat16)
    query_grad = jnp.dot(score_grad, all_feat, preferred_element_type=jnp.float32) * score_scale
    images = img_count * lax.axis_size("text") * det_size
    feat_terms = lax.dot_general(
        score_grad, flat_queries, (((0,), (0,)), ((), ())), preferred_element_type=jnp.float32
    ) * (score_scale / images)
    feat_owned = lax.psum_scatter(
        feat_terms.astype(jnp.bfloat16), "text", scatter_dimension=0, tiled=True
    ).astype(jnp.float32)
    feat_grad = lax.psum(feat_owned, "det")
    proj_part = jnp.dot(
        pooled_low.astype(jnp.float32).T, feat_grad, precision=lax.Precision.HIGHEST
    )
    proj_grad = lax.psum(proj_part.astype(jnp.bfloat16), "text").astype(jnp.float32)
    pooled_share_grad = jnp.dot(
        feat_grad, w_proj.astype(jnp.float32).T, precision=lax.Precision.HIGHEST
    )
    pooled_whole_grad = lax.all_gather(pooled_share_grad, "det", axis=1, tiled=True)
    final_grad = (pooled_whole_grad[:, None, :] * pool_weight[:, :, None]).reshape(
        tok_rows, model_width
    )
    hat_grad = final_grad * final_gain
    mean_first = jnp.mean(hat_grad, axis=1, keepdims=True)
    mean_second = jnp.mean(hat_grad * out_hat, axis=1, keepdims=True)
    out_grad = ((hat_grad - mean_first - out_hat * mean_second) * inv_scale).astype(jnp.bfloat16)
    down_terms = lax.dot_general(
        hidden, out_grad, (((0,), (0,)), ((), ())), preferred_element_type=jnp.float32
    )
    down_grad = lax.psum_scatter(
        down_terms.astype(jnp.bfloat16), "text", scatter_dimension=1, tiled=True
    ).astype(jnp.float32)
    hidden_grad = lax.dot_general(
        out_grad, w_down, (((1,), (1,)), ((), ())), preferred_element_type=jnp.float32
    )
    pre_grad = act_back(hidden_grad)[0].astype(jnp.bfloat16)
    up_terms = lax.dot_general(
        normed, pre_grad, (((0,), (0,)), ((), ())), preferred_element_type=jnp.float32
    )
    up_grad = lax.psum_scatter(
        up_terms.astype(jnp.bfloat16), "text", scatter_dimension=0, tiled=True
    ).astype(jnp.float32)
    return (up_grad, down_grad, proj_grad, query_grad.reshape(img_count, query_count, query_width))


def body(
    prompt_embeds, prompt_len, norm_gain, w_up, w_down, final_gain, w_proj, queries, assign, valid
):
    per_group, prompt, width = prompt_embeds.shape
    tok_rows = per_group * prompt
    det_size = lax.axis_size("det")
    text_size = lax.axis_size("text")
    det = lax.axis_index("det")
    text = lax.axis_index("text")
    if 4 * text_size * tok_rows * width * 2 > ROOM:
        return body_scatter(
            prompt_embeds, prompt_len, norm_gain, w_up, w_down, final_gain, w_proj, queries,
            assign, valid
        )
    share = tok_rows // det_size
    cols = width // text_size
    others = list(range(1, text_size))

    tokens = prompt_embeds.reshape(tok_rows, width).astype(FULL)
    row_mean = jnp.mean(tokens, axis=1, keepdims=True)
    centred = tokens - row_mean
    variance = jnp.mean(centred * centred, axis=1, keepdims=True)
    normed = (centred * lax.rsqrt(variance + EPS) * norm_gain).astype(LOW)

    pre_act = dot_n(normed, w_up)
    hidden, slope = gelu_both(pre_act)
    partial = dot_n(hidden, w_down).astype(LOW)
    summed = scatter_det(partial.reshape(det_size, share, width), det)

    piece = lax.dynamic_slice_in_dim(normed, det * share, share, 0)
    normed_far = jnp.stack([swap(piece, "text", a) for a in others])
    normed_far, offsets = gather_det(normed_far)
    far_rows = det_size * len(others) * share
    normed_far = normed_far.reshape(far_rows, width)
    proj_all, _ = gather_det(w_proj)
    order = det ^ jnp.argsort(jnp.array(offsets)).astype(jnp.int32)
    inverse = jnp.array(offsets).argsort().astype(jnp.int32)[
        det ^ jnp.arange(det_size, dtype=jnp.int32)
    ]
    del order
    proj_all = jnp.take(proj_all, inverse, axis=0).reshape(width, w_proj.shape[1])

    base = det * share
    own_tokens = lax.dynamic_slice_in_dim(
        prompt_embeds.reshape(tok_rows, width), base, share, 0
    ).astype(FULL)
    layer_out = own_tokens + summed
    out_mean = jnp.mean(layer_out, axis=1, keepdims=True)
    out_centred = layer_out - out_mean
    out_var = jnp.mean(out_centred * out_centred, axis=1, keepdims=True)
    inv_scale = lax.rsqrt(out_var + EPS)
    row_id = base + lax.iota(jnp.int32, share)
    row_len = jnp.take(prompt_len, row_id // prompt)
    used = (row_id % prompt < row_len).astype(FULL)
    inv_high = inv_scale[:, 0].astype(LOW)
    inv_low = (inv_scale[:, 0] - inv_high.astype(FULL)).astype(LOW)
    extras = jnp.stack(
        [inv_high, inv_low, used.astype(LOW), row_len.astype(LOW)], axis=1
    )
    extras = jnp.pad(extras, ((0, 0), (0, PACK - extras.shape[1])))
    packed = jnp.concatenate([(out_centred * inv_scale).astype(LOW), extras], axis=1)
    packed_near, _ = gather_det(packed)
    packed_near = packed_near.reshape(tok_rows, width + PACK)
    packed_far = jnp.stack([swap(packed, "text", a) for a in others])
    packed_far, _ = gather_det(packed_far)
    packed_far = packed_far.reshape(far_rows, width + PACK)

    def row_facts(packed_rows, sources):
        at = (det ^ jnp.array(offsets, jnp.int32))[:, None, None] * share
        at = at + lax.iota(jnp.int32, share)[None, None, :]
        concept = at // prompt + jnp.array(sources, jnp.int32)[None, :, None] * per_group
        concept = concept.reshape(-1)
        facts = packed_rows[:, width : width + 4].astype(FULL)
        inv = facts[:, 0] + facts[:, 1]
        pool = facts[:, 2] / facts[:, 3]
        every = text_size * per_group
        pick = concept[:, None] == lax.iota(jnp.int32, every)[None, :]
        return inv, pool, facts[:, 2], pick

    near = row_facts(packed_near, [0])
    far = row_facts(packed_far, others)
    hat_near = packed_near[:, :width]
    hat_far = packed_far[:, :width]

    near_used = (near[3][:, :per_group] & (near[2] > 0)[:, None]).astype(LOW)
    count = jnp.sum(near_used.astype(FULL), axis=0)
    pooled_sum = dot_c(near_used, hat_near)
    pooled = (pooled_sum * final_gain / count[:, None]).astype(LOW)
    concept_feat = dot_n(pooled, proj_all).astype(LOW)
    all_feat = jnp.concatenate(
        [concept_feat] + [swap(concept_feat, "text", a) for a in others], 0
    )

    concept_count = all_feat.shape[0]
    img_count, query_count, query_width = queries.shape
    query_rows = img_count * query_count
    flat_queries = queries.reshape(query_rows, query_width)
    score_scale = query_width ** (-0.5)
    scores = dot_t(flat_queries, all_feat) * score_scale + LOGIT_BIAS
    slots = lax.iota(jnp.int32, concept_count)
    column = (text ^ (slots // per_group)) * per_group + slots % per_group
    target = (assign[:, :, None] == column).astype(FULL).reshape(query_rows, concept_count)
    blocks = valid.astype(FULL).reshape(img_count, text_size, per_group)
    allowed = jnp.take(
        blocks, text ^ jnp.arange(text_size, dtype=jnp.int32), axis=1
    ).reshape(img_count, 1, concept_count)
    weight = jnp.broadcast_to(allowed, (img_count, query_count, concept_count)).reshape(
        query_rows, concept_count
    )
    score_grad = jax.grad(focal_total)(scores, target, weight).astype(LOW)
    query_grad = dot_n(score_grad, all_feat) * score_scale
    images = img_count * text_size * det_size
    terms = dot_c(score_grad, flat_queries) * (score_scale / images)

    terms = terms.astype(LOW).reshape(text_size, per_group, query_width)
    total = terms.astype(FULL)
    for a in others:
        send = jnp.stack([terms[a ^ b] for b in range(text_size)])
        total = total + swap(send, "text", a).astype(FULL)
    feat_grad = sum_det(total.astype(LOW).reshape(concept_count, query_width))
    feat_low = feat_grad.astype(LOW)

    scaled_proj = proj_all.astype(FULL) * final_gain[:, None]
    scaled_proj = (scaled_proj - jnp.mean(scaled_proj, axis=0, keepdims=True)).astype(LOW)
    to_hidden = lax.dot_general(
        scaled_proj, w_down, (((0,), (1,)), ((), ())), preferred_element_type=FULL
    ).astype(LOW)
    pre_far = dot_n(normed_far, w_up)
    hidden_far, slope_far = gelu_both(pre_far)
    down_cols = lax.dynamic_slice_in_dim(scaled_proj, text * cols, cols, 0)

    grad_hidden = dot_n(feat_low, to_hidden).astype(LOW)
    grad_cols = dot_t(feat_low, down_cols).astype(LOW)

    def rows_part(facts, hat, normed_rows, hidden_rows, slope_rows):
        inv, pool, _, pick = facts
        back = dot_t(hat, w_down)
        along = dot_n(hat, scaled_proj).astype(LOW)
        chosen = pick.astype(LOW)
        second = jnp.sum(dot_t(along, feat_low) * pick.astype(FULL), axis=1) * pool / width
        lead = (inv * pool)[:, None]
        tail = (inv * second)[:, None]
        pre_grad = (
            slope_rows.astype(FULL) * (lead * dot_n(chosen, grad_hidden) - tail * back)
        ).astype(LOW)
        hat_cols = lax.dynamic_slice_in_dim(hat, text * cols, cols, 1)
        normed_cols = lax.dynamic_slice_in_dim(normed_rows, text * cols, cols, 1)
        out_grad = (
            lead * dot_n(chosen, grad_cols) - tail * hat_cols.astype(FULL)
        ).astype(LOW)
        return dot_c(normed_cols, pre_grad), dot_c(hidden_rows, out_grad)

    order_near = (det ^ jnp.array(offsets, jnp.int32))
    def near_order(values):
        parts = values.reshape(det_size, share, values.shape[1])
        return jnp.take(parts, order_near, axis=0).reshape(values.shape)

    up_near, down_near = rows_part(
        near, hat_near, near_order(normed), near_order(hidden), near_order(slope)
    )
    up_far, down_far = rows_part(far, hat_far, normed_far, hidden_far, slope_far)

    part = width // det_size
    part_gain = lax.dynamic_slice_in_dim(final_gain, det * part, part, 0)

    def pooled_part(facts, hat):
        mask = (facts[3] & (facts[2] > 0)[:, None]).astype(LOW)
        return (
            dot_c(mask, lax.dynamic_slice_in_dim(hat, det * part, part, 1)),
            jnp.sum(mask.astype(FULL), axis=0),
        )

    sum_near, count_near = pooled_part(near, hat_near)
    sum_far, count_far = pooled_part(far, hat_far)
    pooled_all = (sum_near + sum_far) * part_gain / (count_near + count_far)[:, None]
    proj_grad = lax.dot_general(
        pooled_all.astype(LOW).astype(FULL),
        feat_grad,
        (((0,), (0,)), ((), ())),
        precision=lax.Precision.HIGHEST,
    )
    return (
        up_near + up_far,
        down_near + down_far,
        proj_grad,
        query_grad.reshape(img_count, query_count, query_width),
    )


def solution(mesh):
    return jax.shard_map(
        body,
        mesh=mesh,
        in_specs=(
            P("text", None, None),
            P("text"),
            P(),
            P(None, "det"),
            P("det", None),
            P(),
            P("det", None),
            P(("text", "det"), None, None),
            P(("text", "det"), None),
            P(("text", "det"), None),
        ),
        out_specs=(
            P("text", "det"),
            P("det", "text"),
            P("det", None),
            P(("text", "det"), None, None),
        ),
        check_vma=False,
    )
```

```python
import jax
import jax.numpy as jnp
from jax import lax
from jax.experimental import pallas as pl
from jax.experimental.pallas import tpu as pltpu
from jax.sharding import PartitionSpec as P

EPS = 1e-05
ALPHA = 0.25
LOGIT_BIAS = -2.0
PACK = 128
ROOM = 24 << 20
LOW = jnp.bfloat16
FULL = jnp.float32


def gelu_fn(values):
    return jax.nn.gelu(values, approximate=True)


def gelu_both(values):
    act, slope = jax.jvp(gelu_fn, (values,), (jnp.ones_like(values),))
    return act.astype(LOW), slope.astype(LOW)


def focal_total(scores, target, weight):
    log_pos = jax.nn.log_sigmoid(scores)
    log_neg = jax.nn.log_sigmoid(-scores)
    probab = jax.nn.sigmoid(scores)
    pos_term = -ALPHA * target * (1.0 - probab) ** 2 * log_pos
    neg_term = -(1.0 - ALPHA) * (1.0 - target) * probab**2 * log_neg
    return jnp.sum(weight * (pos_term + neg_term))


def swap(values, axis, mask):
    size = lax.axis_size(axis)
    return lax.ppermute(values, axis, [(i, i ^ mask) for i in range(size)])


def bit_groups(size):
    bits = size.bit_length() - 1
    assert size == 1 << bits
    groups = [[0, 1]] if bits else []
    bit = 1
    while bit < bits:
        wide = min(2, bits - bit)
        groups.append([k << bit for k in range(1 << wide)])
        bit += wide
    return groups


def gather_pieces(values):
    pieces, offsets = [values], [0]
    groups = bit_groups(lax.axis_size("det"))
    for masks in groups[1:] + groups[:1]:
        pieces = pieces + [swap(p, "det", m) for m in masks[1:] for p in pieces]
        offsets = [m ^ o for m in masks for o in offsets]
    return pieces, offsets


def sum_det(values):
    for masks in bit_groups(lax.axis_size("det")):
        total = values.astype(FULL)
        for m in masks[1:]:
            total = total + swap(values, "det", m).astype(FULL)
        values = total.astype(LOW)
    return total


def scatter_det(values, index):
    for masks in bit_groups(lax.axis_size("det")):
        wide = len(masks)
        here = lax.rem(index, wide)
        index = lax.div(index, wide)
        split = values.reshape((values.shape[0] // wide, wide) + values.shape[1:])
        total = lax.dynamic_index_in_dim(split, here, 1, keepdims=False).astype(FULL)
        for n, m in enumerate(masks[1:], 1):
            away = lax.dynamic_index_in_dim(split, here ^ n, 1, keepdims=False)
            total = total + swap(away, "det", m).astype(FULL)
        values = total.astype(LOW)
    return total[0]


def dot_t(left, right):
    return lax.dot_general(left, right, (((1,), (1,)), ((), ())), preferred_element_type=FULL)


def dot_c(left, right):
    return lax.dot_general(left, right, (((0,), (0,)), ((), ())), preferred_element_type=FULL)


def dot_n(left, right):
    return jnp.dot(left, right, preferred_element_type=FULL)


def whole(array):
    return pl.BlockSpec(array.shape, lambda *_: (0,) * len(array.shape))


def call(kernel, grid, scalars, operands, in_specs, out_shapes, out_specs, scratch, flops, name):
    moved = sum(a.size * a.dtype.itemsize for a in operands)
    moved += sum(o.size * o.dtype.itemsize for o in out_shapes)
    return pl.pallas_call(
        kernel,
        out_shape=out_shapes,
        grid_spec=pltpu.PrefetchScalarGridSpec(
            num_scalar_prefetch=1,
            grid=grid,
            in_specs=in_specs,
            out_specs=out_specs,
            scratch_shapes=scratch,
        ),
        compiler_params=pltpu.CompilerParams(dimension_semantics=("arbitrary",) * len(grid)),
        cost_estimate=pl.CostEstimate(flops=flops, bytes_accessed=moved, transcendentals=0),
        name=name,
    )(scalars, *operands)


def shape(dims, dtype=LOW):
    return jax.ShapeDtypeStruct(dims, dtype)


def front(tokens, norm_gain, w_up, w_down, scalars):
    rows, width = tokens.shape
    units = w_up.shape[1]
    step = min(256, units)

    def kernel(scal, tok, gain, up, down, normed, hidden, slope, partial, acc):
        n = pl.program_id(0)

        @pl.when(n == 0)
        def _():
            x = tok[...].astype(FULL)
            centred = x - jnp.mean(x, axis=1, keepdims=True)
            var = jnp.mean(centred * centred, axis=1, keepdims=True)
            normed[...] = (centred * lax.rsqrt(var + EPS) * gain[...]).astype(LOW)
            acc[...] = jnp.zeros_like(acc)

        act, slp = gelu_both(dot_n(normed[...], up[...]))
        hidden[...] = act
        slope[...] = slp
        acc[...] += dot_n(act, down[...])

        @pl.when(n == pl.num_programs(0) - 1)
        def _():
            partial[...] = acc[...].astype(LOW)

    gain = norm_gain[None, :]
    outs = [shape((rows, width)), shape((rows, units)), shape((rows, units)), shape((rows, width))]
    return call(
        kernel,
        (units // step,),
        scalars,
        (tokens, gain, w_up, w_down),
        [
            whole(tokens),
            whole(gain),
            pl.BlockSpec((width, step), lambda n, _: (0, n)),
            pl.BlockSpec((step, width), lambda n, _: (n, 0)),
        ],
        outs,
        [
            whole(outs[0]),
            pl.BlockSpec((rows, step), lambda n, _: (0, n)),
            pl.BlockSpec((rows, step), lambda n, _: (0, n)),
            whole(outs[3]),
        ],
        [pltpu.VMEM((rows, width), FULL)],
        4 * rows * width * units,
        "front",
    )


def fill(scal, pieces, offsets, held, share):
    sources = pieces[0].shape[0]
    rows = len(pieces) * share
    for piece, offset in zip(pieces, offsets):
        place = (scal[0] ^ offset) * share
        for a in range(sources):
            at = pl.multiple_of(a * rows + place, share)
            held[pl.ds(at, share), :] = piece[a]


def far_front(pieces, offsets, w_up, scalars, cols):
    sources, share, width = pieces[0].shape
    rows = sources * share * len(pieces)
    units = w_up.shape[1]
    step = min(256, units)
    count = len(pieces)

    def kernel(scal, *refs):
        up = refs[count]
        hidden, slope, part, held = refs[count + 1 :]

        @pl.when(pl.program_id(0) == 0)
        def _():
            fill(scal, refs[:count], offsets, held, share)
            part[...] = held[:, pl.ds(pl.multiple_of(scal[1] * cols, 128), cols)]

        act, slp = gelu_both(dot_n(held[...], up[...]))
        hidden[...] = act
        slope[...] = slp

    outs = [shape((rows, units)), shape((rows, units)), shape((rows, cols))]
    return call(
        kernel,
        (units // step,),
        scalars,
        (*pieces, w_up),
        [whole(p) for p in pieces] + [pl.BlockSpec((width, step), lambda n, _: (0, n))],
        outs,
        [
            pl.BlockSpec((rows, step), lambda n, _: (0, n)),
            pl.BlockSpec((rows, step), lambda n, _: (0, n)),
            whole(outs[2]),
        ],
        [pltpu.VMEM((rows, width), LOW)],
        2 * rows * width * units,
        "far_front",
    )


def concept_side(pieces, proj_pieces, offsets, lengths, final_gain, scalars, prompt):
    _, share, packed = pieces[0].shape
    rows = share * len(pieces)
    part, query_width = proj_pieces[0].shape
    width = part * len(pieces)
    concepts = lengths.shape[0]
    count = len(pieces)

    def kernel(scal, *refs):
        near, proj = refs[:count], refs[count : 2 * count]
        lens, gain, gain_t = refs[2 * count : 2 * count + 3]
        hat, feat, pooled_part, centred, full_proj = refs[2 * count + 3 :]
        fill(scal, near, offsets, hat, share)
        for piece, offset in zip(proj, offsets):
            at = pl.multiple_of((scal[0] ^ offset) * part, part)
            full_proj[pl.ds(at, part), :] = piece[...]
        row = lax.broadcasted_iota(jnp.int32, (concepts, rows), 1)
        concept = lax.broadcasted_iota(jnp.int32, (concepts, rows), 0)
        low = concept * prompt
        pick = (row >= low) & (row < low + lens[...])
        pick = jnp.where(pick, 1.0, 0.0).astype(LOW)
        pooled = dot_n(pick, hat[:, :width]) * gain[...] / lens[...].astype(FULL)
        full_proj_now = full_proj[...]
        pooled_low = pooled.astype(LOW)
        feat[...] = dot_n(pooled_low, full_proj_now).astype(LOW)
        pooled_all[...] = pooled_low
        pooled_part[...] = pooled_all[:, pl.ds(pl.multiple_of(scal[0] * part, 128), part)]
        scaled = full_proj_now.astype(FULL) * gain_t[...]
        centred[...] = (scaled - jnp.mean(scaled, axis=0, keepdims=True)).astype(LOW)

    def outer(scal, *refs):
        nonlocal pooled_all
        pooled_all = refs[-1]
        kernel(scal, *refs[:-1])

    pooled_all = None
    gain = final_gain[None, :]
    gain_t = final_gain[:, None]
    outs = [
        shape((rows, packed)),
        shape((concepts, query_width)),
        shape((concepts, part)),
        shape((width, query_width)),
    ]
    operands = (*pieces, *proj_pieces, lengths, gain, gain_t)
    return call(
        outer,
        (1,),
        scalars,
        operands,
        [whole(o) for o in operands],
        outs,
        [whole(o) for o in outs],
        [pltpu.VMEM((width, query_width), LOW), pltpu.VMEM((concepts, width), LOW)],
        2 * concepts * width * (rows + query_width),
        "concept_side",
    )


def back_side(pieces, offsets, w_down, centred, scalars, cols):
    sources, share, packed = pieces[0].shape
    rows = sources * share * len(pieces)
    units, width = w_down.shape
    query_width = centred.shape[1]
    step = min(256, units)
    count = len(pieces)

    def kernel(scal, *refs):
        down, proj = refs[count : count + 2]
        back, along, part, facts, held = refs[count + 2 :]

        @pl.when(pl.program_id(0) == 0)
        def _():
            fill(scal, refs[:count], offsets, held, share)
            part[...] = held[:, pl.ds(pl.multiple_of(scal[1] * cols, 128), cols)]
            facts[...] = held[:, width:]
            along[...] = dot_n(held[:, :width], proj[...]).astype(LOW)

        back[...] = dot_t(held[:, :width], down[...]).astype(LOW)

    outs = [
        shape((rows, units)),
        shape((rows, query_width)),
        shape((rows, cols)),
        shape((rows, packed - width)),
    ]
    return call(
        kernel,
        (units // step,),
        scalars,
        (*pieces, w_down, centred),
        [whole(p) for p in pieces]
        + [pl.BlockSpec((step, width), lambda n, _: (n, 0)), whole(centred)],
        outs,
        [
            pl.BlockSpec((rows, step), lambda n, _: (0, n)),
            whole(outs[1]),
            whole(outs[2]),
            whole(outs[3]),
        ],
        [pltpu.VMEM((rows, packed), LOW)],
        2 * rows * width * (units + query_width),
        "back_side",
    )


def late(feat_low, to_hidden, centred_cols, near, far, scalars, prompt):
    near_rows, far_rows = near[0].shape[0], far[0].shape[0]
    units = to_hidden.shape[1]
    cols = near[5].shape[1]
    width = None
    concepts, query_width = feat_low.shape
    step = min(256, units)
    model = lax.axis_size("text") * cols

    def one(refs, first, feat, grad_step, grad_cols, out_grad, weights, start):
        facts, along, back, slope, hidden, hat_cols, normed_cols = refs
        rows = facts.shape[0]
        row = lax.broadcasted_iota(jnp.int32, (rows, concepts), 0) + start
        low = lax.broadcasted_iota(jnp.int32, (rows, concepts), 1) * prompt
        pick = jnp.where((row >= low) & (row < low + prompt), 1.0, 0.0).astype(LOW)
        span = pl.ds(start, rows)

        @pl.when(first)
        def _():
            known = facts[...].astype(FULL)
            inv = known[:, 0:1] + known[:, 1:2]
            pool = known[:, 2:3] / known[:, 3:4]
            chosen = dot_n(pick, feat[...])
            second = jnp.sum(along[...].astype(FULL) * chosen, axis=1, keepdims=True)
            lead = inv * pool
            tail = lead * second * (1.0 / model)
            weights[span, 0:1] = lead
            weights[span, 1:2] = tail
            out_grad[span, :] = (
                lead * dot_n(pick, grad_cols) - tail * hat_cols[...].astype(FULL)
            ).astype(LOW)

        lead = weights[span, 0:1]
        tail = weights[span, 1:2]
        pre_grad = (
            slope[...].astype(FULL)
            * (lead * dot_n(pick, grad_step) - tail * back[...].astype(FULL))
        ).astype(LOW)
        return (
            dot_c(normed_cols[...], pre_grad),
            dot_c(hidden[...], out_grad[span, :]),
        )

    def kernel(scal, *refs):
        feat, hid, ccols = refs[:3]
        near_refs, far_refs = refs[3:10], refs[10:17]
        up, down, out_grad, weights = refs[17:]
        first = pl.program_id(0) == 0
        grad_step = dot_n(feat[...], hid[...]).astype(LOW)
        grad_cols = dot_t(feat[...], ccols[...]).astype(LOW)
        up_a, down_a = one(near_refs, first, feat, grad_step, grad_cols, out_grad, weights, 0)
        up_b, down_b = one(
            far_refs, first, feat, grad_step, grad_cols, out_grad, weights, near_rows
        )
        up[...] = up_a + up_b
        down[...] = down_a + down_b

    def specs(rows):
        moving = pl.BlockSpec((rows, step), lambda n, _: (0, n))
        return moving

    in_specs = [whole(feat_low), pl.BlockSpec((query_width, step), lambda n, _: (0, n)), whole(centred_cols)]
    for part in (near, far):
        in_specs += [whole(part[0]), whole(part[1])]
        in_specs += [specs(part[0].shape[0])] * 3
        in_specs += [whole(part[5]), whole(part[6])]
    outs = [shape((cols, units), FULL), shape((units, cols), FULL)]
    return call(
        kernel,
        (units // step,),
        scalars,
        (feat_low, to_hidden, centred_cols, *near, *far),
        in_specs,
        outs,
        [
            pl.BlockSpec((cols, step), lambda n, _: (0, n)),
            pl.BlockSpec((step, cols), lambda n, _: (n, 0)),
        ],
        [
            pltpu.VMEM((near_rows + far_rows, cols), LOW),
            pltpu.VMEM((near_rows + far_rows, 128), FULL),
        ],
        4 * (near_rows + far_rows) * units * cols,
        "late",
    )


def body_scatter(
    prompt_embeds, prompt_len, norm_gain, w_up, w_down, final_gain, w_proj, queries, assign, valid
):
    per_group, prompt, model_width = prompt_embeds.shape
    tok_rows = per_group * prompt
    det_size = lax.axis_size("det")
    share = model_width // det_size
    offset = lax.axis_index("det") * share
    tokens = prompt_embeds.reshape(tok_rows, model_width).astype(jnp.float32)
    row_mean = jnp.mean(tokens, axis=1, keepdims=True)
    centred = tokens - row_mean
    variance = jnp.mean(centred * centred, axis=1, keepdims=True)
    normed = (centred * lax.rsqrt(variance + EPS) * norm_gain).astype(jnp.bfloat16)
    pre_act = jnp.dot(normed, w_up, preferred_element_type=jnp.float32)
    hidden_act, act_back = jax.vjp(gelu_fn, pre_act)
    hidden = hidden_act.astype(jnp.bfloat16)
    partial_out = jnp.dot(hidden, w_down, preferred_element_type=jnp.float32)
    position = lax.broadcasted_iota(jnp.int32, (per_group, prompt), 1)
    lengths = prompt_len.astype(jnp.float32)
    pool_weight = (position < prompt_len[:, None]).astype(jnp.float32) / lengths[:, None]
    layer_out = tokens + lax.psum(partial_out.astype(jnp.bfloat16), "det").astype(jnp.float32)
    out_mean = jnp.mean(layer_out, axis=1, keepdims=True)
    out_centred = layer_out - out_mean
    out_var = jnp.mean(out_centred * out_centred, axis=1, keepdims=True)
    inv_scale = lax.rsqrt(out_var + EPS)
    out_hat = out_centred * inv_scale
    final = out_hat * final_gain
    pooled_full = jnp.sum(
        final.reshape(per_group, prompt, model_width) * pool_weight[:, :, None], axis=1
    )
    pooled_share = lax.dynamic_slice_in_dim(pooled_full, offset, share, 1)
    pooled_low = pooled_share.astype(jnp.bfloat16)
    feat_part = jnp.dot(pooled_low, w_proj, preferred_element_type=jnp.float32)
    concept_feat = lax.psum(feat_part, "det").astype(jnp.bfloat16)
    all_feat = lax.all_gather(concept_feat, "text", axis=0, tiled=True)
    concept_count = all_feat.shape[0]
    img_count, query_count, query_width = queries.shape
    query_rows = img_count * query_count
    flat_queries = queries.reshape(query_rows, query_width)
    score_scale = query_width ** (-0.5)
    scores = (
        lax.dot_general(
            flat_queries, all_feat, (((1,), (1,)), ((), ())), preferred_element_type=jnp.float32
        )
        * score_scale
        + LOGIT_BIAS
    )
    column = lax.broadcasted_iota(jnp.int32, (img_count, query_count, concept_count), 2)
    target = (assign[:, :, None] == column).astype(jnp.float32).reshape(query_rows, concept_count)
    weight = jnp.broadcast_to(
        valid[:, None, :].astype(jnp.float32), (img_count, query_count, concept_count)
    ).reshape(query_rows, concept_count)
    score_grad = jax.grad(focal_total)(scores, target, weight).astype(jnp.bfloat16)
    query_grad = jnp.dot(score_grad, all_feat, preferred_element_type=jnp.float32) * score_scale
    images = img_count * lax.axis_size("text") * det_size
    feat_terms = lax.dot_general(
        score_grad, flat_queries, (((0,), (0,)), ((), ())), preferred_element_type=jnp.float32
    ) * (score_scale / images)
    feat_owned = lax.psum_scatter(
        feat_terms.astype(jnp.bfloat16), "text", scatter_dimension=0, tiled=True
    ).astype(jnp.float32)
    feat_grad = lax.psum(feat_owned, "det")
    proj_part = jnp.dot(
        pooled_low.astype(jnp.float32).T, feat_grad, precision=lax.Precision.HIGHEST
    )
    proj_grad = lax.psum(proj_part.astype(jnp.bfloat16), "text").astype(jnp.float32)
    pooled_share_grad = jnp.dot(
        feat_grad, w_proj.astype(jnp.float32).T, precision=lax.Precision.HIGHEST
    )
    pooled_whole_grad = lax.all_gather(pooled_share_grad, "det", axis=1, tiled=True)
    final_grad = (pooled_whole_grad[:, None, :] * pool_weight[:, :, None]).reshape(
        tok_rows, model_width
    )
    hat_grad = final_grad * final_gain
    mean_first = jnp.mean(hat_grad, axis=1, keepdims=True)
    mean_second = jnp.mean(hat_grad * out_hat, axis=1, keepdims=True)
    out_grad = ((hat_grad - mean_first - out_hat * mean_second) * inv_scale).astype(jnp.bfloat16)
    down_terms = lax.dot_general(
        hidden, out_grad, (((0,), (0,)), ((), ())), preferred_element_type=jnp.float32
    )
    down_grad = lax.psum_scatter(
        down_terms.astype(jnp.bfloat16), "text", scatter_dimension=1, tiled=True
    ).astype(jnp.float32)
    hidden_grad = lax.dot_general(
        out_grad, w_down, (((1,), (1,)), ((), ())), preferred_element_type=jnp.float32
    )
    pre_grad = act_back(hidden_grad)[0].astype(jnp.bfloat16)
    up_terms = lax.dot_general(
        normed, pre_grad, (((0,), (0,)), ((), ())), preferred_element_type=jnp.float32
    )
    up_grad = lax.psum_scatter(
        up_terms.astype(jnp.bfloat16), "text", scatter_dimension=0, tiled=True
    ).astype(jnp.float32)
    return (up_grad, down_grad, proj_grad, query_grad.reshape(img_count, query_count, query_width))


def body(
    prompt_embeds, prompt_len, norm_gain, w_up, w_down, final_gain, w_proj, queries, assign, valid
):
    per_group, prompt, width = prompt_embeds.shape
    tok_rows = per_group * prompt
    det_size = lax.axis_size("det")
    text_size = lax.axis_size("text")
    det = lax.axis_index("det")
    text = lax.axis_index("text")
    if 4 * text_size * tok_rows * width * 2 > ROOM:
        return body_scatter(
            prompt_embeds, prompt_len, norm_gain, w_up, w_down, final_gain, w_proj, queries,
            assign, valid
        )
    share = tok_rows // det_size
    cols = width // text_size
    others = list(range(1, text_size))
    scalars = jnp.stack([det, text]).astype(jnp.int32)
    flat_tokens = prompt_embeds.reshape(tok_rows, width)
    own_tokens = lax.dynamic_slice_in_dim(flat_tokens, det * share, share, 0).astype(FULL)

    row_mean = jnp.mean(own_tokens, axis=1, keepdims=True)
    centred = own_tokens - row_mean
    variance = jnp.mean(centred * centred, axis=1, keepdims=True)
    piece = (centred * lax.rsqrt(variance + EPS) * norm_gain).astype(LOW)
    normed_far = jnp.stack([swap(piece, "text", a) for a in others])
    far_pieces, offsets = gather_pieces(normed_far)
    proj_pieces, _ = gather_pieces(w_proj)

    normed, hidden, slope, partial = front(flat_tokens, norm_gain, w_up, w_down, scalars)
    summed = scatter_det(partial.reshape(det_size, share, width), det)

    layer_out = own_tokens + summed
    out_mean = jnp.mean(layer_out, axis=1, keepdims=True)
    out_centred = layer_out - out_mean
    out_var = jnp.mean(out_centred * out_centred, axis=1, keepdims=True)
    inv_scale = lax.rsqrt(out_var + EPS)
    spread = jnp.broadcast_to(prompt_len[:, None], (per_group, prompt)).reshape(tok_rows, 1)
    place = lax.broadcasted_iota(jnp.int32, (per_group, prompt), 1).reshape(tok_rows, 1)
    known = jnp.concatenate([(place < spread).astype(FULL), spread.astype(FULL)], 1)
    known = lax.dynamic_slice_in_dim(known, det * share, share, 0)
    inv_high = inv_scale.astype(LOW).astype(FULL)
    lane = lax.broadcasted_iota(jnp.int32, (share, PACK), 1)
    extras = jnp.where(lane == 0, inv_high, 0.0)
    extras = jnp.where(lane == 1, inv_scale - inv_high, extras)
    extras = jnp.where(lane == 2, known[:, 0:1], extras)
    extras = jnp.where(lane == 3, known[:, 1:2], extras)
    packed = jnp.concatenate([out_centred * inv_scale, extras], axis=1).astype(LOW)
    near_pieces, _ = gather_pieces(packed[None])
    packed_far = jnp.stack([swap(packed, "text", a) for a in others])
    far_packed, _ = gather_pieces(packed_far)

    hat_near, concept_feat, pooled_part, scaled_proj = concept_side(
        near_pieces, proj_pieces, offsets, prompt_len[:, None], final_gain, scalars, prompt
    )
    feats = jnp.concatenate([concept_feat, pooled_part], axis=1)
    feats = [feats] + [swap(feats, "text", a) for a in others]
    query_width = queries.shape[2]
    all_feat = jnp.concatenate([f[:, :query_width] for f in feats], 0)
    pooled_all = jnp.concatenate([f[:, query_width:] for f in feats], 0)

    concept_count = all_feat.shape[0]
    img_count, query_count, query_width = queries.shape
    query_rows = img_count * query_count
    flat_queries = queries.reshape(query_rows, query_width)
    score_scale = query_width ** (-0.5)
    scores = dot_t(flat_queries, all_feat) * score_scale + LOGIT_BIAS
    slots = lax.iota(jnp.int32, concept_count)
    column = (text ^ (slots // per_group)) * per_group + slots % per_group
    target = (assign[:, :, None] == column).astype(FULL).reshape(query_rows, concept_count)
    blocks = valid.astype(FULL).reshape(img_count, text_size, per_group)
    allowed = jnp.concatenate(
        [lax.dynamic_slice_in_dim(blocks, text ^ a, 1, 1) for a in range(text_size)], 1
    ).reshape(img_count, 1, concept_count)
    weight = jnp.broadcast_to(allowed, (img_count, query_count, concept_count)).reshape(
        query_rows, concept_count
    )
    score_grad = jax.grad(focal_total)(scores, target, weight).astype(LOW)
    query_grad = dot_n(score_grad, all_feat) * score_scale
    images = img_count * text_size * det_size
    terms = dot_c(score_grad, flat_queries) * (score_scale / images)

    terms = terms.astype(LOW).reshape(text_size, per_group, query_width)
    total = terms.astype(FULL)
    for a in others:
        send = jnp.stack([terms[a ^ b] for b in range(text_size)])
        total = total + swap(send, "text", a).astype(FULL)
    feat_grad = sum_det(total.astype(LOW).reshape(concept_count, query_width))

    to_hidden = lax.dot_general(
        scaled_proj, w_down, (((0,), (1,)), ((), ())), preferred_element_type=FULL
    ).astype(LOW)
    hidden_far, slope_far, normed_cols_far = far_front(
        far_pieces, offsets, w_up, scalars, cols
    )
    back_near, along_near, hat_cols_near, facts_near = back_side(
        [hat_near[None]], [0], w_down, scaled_proj, jnp.stack([0 * det, text]), cols
    )
    back_far, along_far, hat_cols_far, facts_far = back_side(
        far_packed, offsets, w_down, scaled_proj, scalars, cols
    )
    centred_cols = lax.dynamic_slice_in_dim(scaled_proj, text * cols, cols, 0)
    normed_cols = lax.dynamic_slice_in_dim(normed, text * cols, cols, 1)

    up_grad, down_grad = late(
        feat_grad.astype(LOW),
        to_hidden,
        centred_cols,
        (facts_near, along_near, back_near, slope, hidden, hat_cols_near, normed_cols),
        (facts_far, along_far, back_far, slope_far, hidden_far, hat_cols_far, normed_cols_far),
        scalars,
        prompt,
    )
    proj_grad = lax.dot_general(
        pooled_all.astype(FULL),
        feat_grad,
        (((0,), (0,)), ((), ())),
        precision=lax.Precision.HIGHEST,
    )
    return (up_grad, down_grad, proj_grad, query_grad.reshape(img_count, query_count, query_width))


def solution(mesh):
    return jax.shard_map(
        body,
        mesh=mesh,
        in_specs=(
            P("text", None, None),
            P("text"),
            P(),
            P(None, "det"),
            P("det", None),
            P(),
            P("det", None),
            P(("text", "det"), None, None),
            P(("text", "det"), None),
            P(("text", "det"), None),
        ),
        out_specs=(
            P("text", "det"),
            P("det", "text"),
            P("det", None),
            P(("text", "det"), None, None),
        ),
        check_vma=False,
    )
```

```python
import jax
import jax.numpy as jnp
from jax import lax
from jax.experimental import pallas as pl
from jax.experimental.pallas import tpu as pltpu
from jax.sharding import PartitionSpec as P


EPS = 1e-05
ALPHA = 0.25
LOGIT_BIAS = -2.0
PACK = 128
ROOM = 24 << 20
LOW = jnp.bfloat16
FULL = jnp.float32


GELU_A = 0.7978845608028654
GELU_B = 0.044715 * GELU_A


def gelu_fn(values):
    return jax.nn.gelu(values, approximate=True)


def gelu_half(values):
    square = values * values
    return square, 0.5 + 0.5 * jnp.tanh(values * (GELU_A + GELU_B * square))


def gelu_both(values):
    square, half = gelu_half(values)
    act = values * half
    slope = half + 2.0 * act * (1.0 - half) * (GELU_A + 3.0 * GELU_B * square)
    return act, slope


def focal_total(scores, target, weight):
    log_pos = jax.nn.log_sigmoid(scores)
    log_neg = jax.nn.log_sigmoid(-scores)
    probab = jax.nn.sigmoid(scores)
    pos_term = -ALPHA * target * (1.0 - probab) ** 2 * log_pos
    neg_term = -(1.0 - ALPHA) * (1.0 - target) * probab**2 * log_neg
    return jnp.sum(weight * (pos_term + neg_term))


def swap(values, axis, mask):
    size = lax.axis_size(axis)
    return lax.ppermute(values, axis, [(i, i ^ mask) for i in range(size)])


def bit_groups(size):
    bits = size.bit_length() - 1
    assert size == 1 << bits
    groups = [[0, 1]] if bits else []
    bit = 1
    while bit < bits:
        wide = min(2, bits - bit)
        groups.append([k << bit for k in range(1 << wide)])
        bit += wide
    return groups


def gather_pieces(values):
    pieces, offsets = [values], [0]
    groups = bit_groups(lax.axis_size("det"))
    for masks in groups[1:] + groups[:1]:
        pieces = pieces + [swap(p, "det", m) for m in masks[1:] for p in pieces]
        offsets = [m ^ o for m in masks for o in offsets]
    return pieces, offsets


def sum_det(values):
    for masks in bit_groups(lax.axis_size("det")):
        parts = [values] + [swap(values, "det", m) for m in masks[1:]]
        values = sum(p.astype(FULL) for p in parts).astype(LOW)
    return parts


def dot_t(left, right):
    return lax.dot_general(left, right, (((1,), (1,)), ((), ())), preferred_element_type=FULL)


def dot_c(left, right):
    return lax.dot_general(left, right, (((0,), (0,)), ((), ())), preferred_element_type=FULL)


def dot_n(left, right):
    return jnp.dot(left, right, preferred_element_type=FULL)


def whole(array):
    return pl.BlockSpec(array.shape, lambda *_: (0,) * len(array.shape))


def call(kernel, grid, scalars, operands, in_specs, out_shapes, out_specs, scratch, flops):
    moved = sum(a.size * a.dtype.itemsize for a in operands)
    moved += sum(o.size * o.dtype.itemsize for o in out_shapes)
    return pl.pallas_call(
        kernel,
        out_shape=out_shapes,
        grid_spec=pltpu.PrefetchScalarGridSpec(
            num_scalar_prefetch=1,
            grid=grid,
            in_specs=in_specs,
            out_specs=out_specs,
            scratch_shapes=scratch,
        ),
        compiler_params=pltpu.CompilerParams(dimension_semantics=("arbitrary",) * len(grid)),
        cost_estimate=pl.CostEstimate(flops=flops, bytes_accessed=moved, transcendentals=0),
    )(scalars, *operands)


def shape(dims, dtype=LOW):
    return jax.ShapeDtypeStruct(dims, dtype)


def scatter_parts(parts, index):
    for masks in bit_groups(lax.axis_size("det"))[1:]:
        wide = len(masks)
        here = lax.rem(index, wide)
        index = lax.div(index, wide)
        split = [p.reshape((p.shape[0] // wide, wide) + p.shape[1:]) for p in parts]
        parts = [lax.dynamic_index_in_dim(p, here, 1, keepdims=False) for p in split]
        for n, m in enumerate(masks[1:], 1):
            away = sum(
                lax.dynamic_index_in_dim(p, here ^ n, 1, keepdims=False).astype(FULL)
                for p in split
            )
            parts.append(swap(away.astype(LOW), "det", m))
    return [p[0] for p in parts]


def front(tokens, norm_gain, w_up, w_down, scalars, cols, share, others):
    rows, width = tokens.shape
    units = w_up.shape[1]
    step = min(256, units)
    pairs = rows // share // 2

    def kernel(scal, tok, gain, up, down, near_cols, far_cols, pre_t, keep, send, normed, acc):
        n = pl.program_id(0)

        @pl.when(n == 0)
        def _():
            x = tok[...].astype(FULL)
            centred = x - jnp.mean(x, axis=1, keepdims=True)
            var = jnp.mean(centred * centred, axis=1, keepdims=True)
            normed[...] = (centred * lax.rsqrt(var + EPS) * gain[...]).astype(LOW)
            near_cols[...] = normed[:, pl.ds(pl.multiple_of(scal[1] * cols, 128), cols)]
            mine = pl.ds(pl.multiple_of(scal[0] * share, share), share)
            for a in others:
                at = pl.multiple_of((scal[1] ^ a) * cols, 128)
                far_cols[a - 1] = normed[mine, pl.ds(at, cols)]

        pre = dot_n(normed[...], up[...])
        pre_t[...] = pre.T.astype(LOW)
        _, half = gelu_half(pre)
        part = dot_n((pre * half).astype(LOW), down[...])

        @pl.when(n == 0)
        def _():
            acc[...] = part

        @pl.when(n > 0)
        def _():
            acc[...] += part

        @pl.when(n == pl.num_programs(0) - 1)
        def _():
            core = lax.rem(scal[0], 2)
            for q in range(pairs):
                at = pl.multiple_of((2 * q + core) * share, share)
                keep[q] = acc[pl.ds(at, share), :].astype(LOW)
                at = pl.multiple_of((2 * q + 1 - core) * share, share)
                send[q] = acc[pl.ds(at, share), :].astype(LOW)

    gain = norm_gain[None, :]
    outs = [
        shape((rows, cols)),
        shape((len(others), share, cols)),
        shape((units, rows)),
        shape((pairs, share, width)),
        shape((pairs, share, width)),
    ]
    return call(
        kernel,
        (units // step,),
        scalars,
        (tokens, gain, w_up, w_down),
        [
            whole(tokens),
            whole(gain),
            pl.BlockSpec((width, step), lambda n, _: (0, n)),
            pl.BlockSpec((step, width), lambda n, _: (n, 0)),
        ],
        outs,
        [
            whole(outs[0]),
            whole(outs[1]),
            pl.BlockSpec((step, rows), lambda n, _: (n, 0)),
            whole(outs[3]),
            whole(outs[4]),
        ],
        [pltpu.VMEM((rows, width), LOW), pltpu.VMEM((rows, width), FULL)],
        4 * rows * width * units,
    )


def out_norm(tokens, parts, far_cols, scalars, prompt, concepts):
    share, width = parts[0].shape
    cols = far_cols.shape[2]
    count = len(parts)

    def kernel(scal, tok, *refs):
        summed = refs[0][...].astype(FULL)
        for ref in refs[1:count]:
            summed = summed + ref[...].astype(FULL)
        far, near = refs[count : count + 2]
        away = refs[count + 2 :]
        x = tok[...].astype(FULL) + summed
        centred = x - jnp.mean(x, axis=1, keepdims=True)
        var = jnp.mean(centred * centred, axis=1, keepdims=True)
        inv = lax.rsqrt(var + EPS)
        hat = (centred * inv).astype(LOW)
        row = lax.broadcasted_iota(jnp.int32, (share, PACK), 0) + scal[0] * share
        lane = lax.broadcasted_iota(jnp.int32, (share, PACK), 1)
        place = lax.rem(row, prompt)
        concept = lax.div(row, prompt)
        length = jnp.zeros((share, PACK), jnp.int32)
        for c in range(concepts):
            length = jnp.where(concept == c, scal[2 + c], length)
        high = inv.astype(LOW).astype(FULL)
        extras = jnp.where(lane == 0, high, 0.0)
        extras = jnp.where(lane == 1, inv - high, extras)
        extras = jnp.where((lane == 2) & (place < length), 1.0, extras)
        extras = jnp.where(lane == 3, length.astype(FULL), extras).astype(LOW)
        near[0, :, :width] = hat
        near[0, :, width:] = extras
        for a, ref in enumerate(away):
            ref[:, :width] = hat
            ref[:, width : width + PACK] = extras
            ref[:, width + PACK :] = far[a]

    outs = [
        shape((1, share, width + PACK)),
    ] + [shape((share, width + PACK + cols))] * far_cols.shape[0]
    operands = (tokens, *parts, far_cols)
    return call(
        kernel,
        (1,),
        scalars,
        operands,
        [pl.BlockSpec((share, width), lambda n, scal: (scal[0], 0))]
        + [whole(o) for o in operands[1:]],
        outs,
        [whole(o) for o in outs],
        [],
        20 * share * width,
    )


def fill(scal, pieces, offsets, held, share, start, width):
    sources = pieces[0].shape[0]
    rows = len(pieces) * share
    for piece, offset in zip(pieces, offsets):
        place = (scal[0] ^ offset) * share
        for a in range(sources):
            at = pl.multiple_of(start + a * rows + place, share)
            held[pl.ds(at, share), :] = piece[a, :, :width]


def proj_side(proj_pieces, offsets, w_down, final_gain, scalars):
    part, query_width = proj_pieces[0].shape
    count = len(proj_pieces)
    width = part * count
    units = w_down.shape[0]
    step = min(256, units)

    def kernel(scal, *refs):
        gain, down, proj, centred, hid_t = refs[count:]

        @pl.when(pl.program_id(0) == 0)
        def _():
            for piece, offset in zip(refs[:count], offsets):
                at = pl.multiple_of((scal[0] ^ offset) * part, part)
                proj[pl.ds(at, part), :] = piece[...]
            tall = jnp.broadcast_to(gain[...], (128, width)).T
            tall = jnp.concatenate([tall] * (query_width // 128), axis=1)
            scaled = proj[...].astype(FULL) * tall
            centred[...] = (scaled - jnp.mean(scaled, axis=0, keepdims=True)).astype(LOW)

        hid_t[...] = dot_n(down[...], centred[...]).astype(LOW)

    gain = final_gain[None, :]
    outs = [shape((width, query_width)), shape((width, query_width)), shape((units, query_width))]
    return call(
        kernel,
        (units // step,),
        scalars,
        (*proj_pieces, gain, w_down),
        [whole(p) for p in proj_pieces]
        + [whole(gain), pl.BlockSpec((step, width), lambda n, _: (n, 0))],
        outs,
        [whole(outs[0]), whole(outs[1]), pl.BlockSpec((step, query_width), lambda n, _: (n, 0))],
        [],
        2 * units * width * query_width,
    )


def concept_side(pieces, offsets, proj, lengths, final_gain, scalars, prompt, part):
    _, share, packed = pieces[0].shape
    rows = share * len(pieces)
    width, query_width = proj.shape
    concepts = lengths.shape[0]
    count = len(pieces)

    def kernel(scal, *refs):
        full_proj, lens, gain, hat, feat, pooled = refs[count:]
        fill(scal, refs[:count], offsets, hat, share, 0, packed)
        row = lax.broadcasted_iota(jnp.int32, (concepts, rows), 1)
        low = lax.broadcasted_iota(jnp.int32, (concepts, rows), 0) * prompt
        pick = (row >= low) & (row < low + lens[...])
        pick = jnp.where(pick, 1.0, 0.0).astype(LOW)
        mean = dot_n(pick, hat[:, :width]) * gain[...] / lens[...].astype(FULL)
        pooled[...] = mean.astype(LOW)
        feat[:, :query_width] = dot_n(pooled[...], full_proj[...]).astype(LOW)
        feat[:, query_width:] = pooled[:, pl.ds(pl.multiple_of(scal[0] * part, 128), part)]

    gain = final_gain[None, :]
    outs = [shape((rows, packed)), shape((concepts, query_width + part))]
    operands = (*pieces, proj, lengths, gain)
    return call(
        kernel,
        (1,),
        scalars,
        operands,
        [whole(o) for o in operands],
        outs,
        [whole(o) for o in outs],
        [pltpu.VMEM((concepts, width), LOW)],
        2 * concepts * width * (rows + query_width),
    )


def score_side(queries, assign, allowed, feats, scalars, query_width, images):
    count, width = queries.shape
    groups = len(feats)
    per_group = feats[0].shape[0]
    concepts = groups * per_group
    half = width // 2

    def kernel(scal, query, chosen, allow, *refs):
        grad_q, own, pooled = refs[groups : groups + 3]
        away = refs[groups + 3 :]
        pooled[...] = jnp.concatenate([r[:, query_width:] for r in refs[:groups]], axis=0)
        feat = jnp.concatenate([r[:, :query_width] for r in refs[:groups]], axis=0)
        scores = dot_t(feat, query[...]) * query_width ** (-0.5) + LOGIT_BIAS
        slot = lax.broadcasted_iota(jnp.int32, (concepts, 1), 0)
        ident = (scal[1] ^ lax.div(slot, per_group)) * per_group + lax.rem(slot, per_group)
        small = jnp.exp(-jnp.abs(scores))
        logs = jnp.log1p(small)
        over = 1.0 / (1.0 + small)
        under = small * over
        up = scores >= 0
        prob = jnp.where(up, over, under)
        rest = jnp.where(up, under, over)
        log_pos = jnp.minimum(scores, 0.0) - logs
        log_neg = jnp.minimum(-scores, 0.0) - logs
        pos = ALPHA * rest * rest * (2.0 * prob * log_pos - rest)
        neg = (1.0 - ALPHA) * prob * prob * (prob - 2.0 * rest * log_neg)
        grad = jnp.where(chosen[...] == ident, pos, neg) * allow[...]
        grad = grad.astype(LOW)
        terms = dot_n(grad, query[...]) * (query_width ** (-0.5) / images)
        terms = terms.astype(LOW)
        own[...] = terms
        for a in range(1, groups):
            for b in range(groups):
                block = (a ^ b) * per_group
                away[a - 1][b * per_group : (b + 1) * per_group, :] = terms[
                    block : block + per_group
                ]
        back = dot_c(grad, feat) * query_width ** (-0.5)
        grad_q[pl.ds(0, count, 2), :] = back[:, :half]
        grad_q[pl.ds(1, count, 2), :] = back[:, half:]

    outs = [
        shape((2 * count, half), FULL),
        shape((concepts, width)),
        shape((concepts, feats[0].shape[1] - query_width)),
    ] + [shape((concepts, width))] * (groups - 1)
    operands = (queries, assign, allowed, *feats)
    return call(
        kernel,
        (1,),
        scalars,
        operands,
        [whole(o) for o in operands],
        outs,
        [whole(o) for o in outs],
        [],
        6 * count * width * concepts,
    )


def back_side(hat_near, cols_near, pieces, offsets, w_down, centred, scalars, cols):
    sources, share, _ = pieces[0].shape
    near_rows, hat_width = hat_near.shape
    rows = near_rows + sources * share * len(pieces)
    units, width = w_down.shape
    query_width = centred.shape[1]
    step = min(256, units)
    count = len(pieces)

    def kernel(scal, near, near_cols, *refs):
        down, proj = refs[count : count + 2]
        back_t, along, part, facts, normed_t, held, held_cols = refs[count + 2 :]

        @pl.when(pl.program_id(0) == 0)
        def _():
            held[:near_rows, :] = near[...]
            held_cols[:near_rows, :] = near_cols[...]
            for piece, offset in zip(refs[:count], offsets):
                place = (scal[0] ^ offset) * share
                for a in range(sources):
                    at = pl.multiple_of(near_rows + a * share * count + place, share)
                    held[pl.ds(at, share), :] = piece[a, :, :hat_width]
                    held_cols[pl.ds(at, share), :] = piece[a, :, hat_width:]
            part[...] = held[:, pl.ds(pl.multiple_of(scal[1] * cols, 128), cols)]
            facts[...] = held[:, width:]
            along[...] = dot_n(held[:, :width], proj[...]).astype(LOW)
            normed_t[...] = held_cols[...].T

        back_t[...] = dot_t(down[...], held[:, :width]).astype(LOW)

    outs = [
        shape((units, rows)),
        shape((rows, query_width)),
        shape((rows, cols)),
        shape((rows, hat_width - width)),
        shape((cols, rows)),
    ]
    operands = (hat_near, cols_near, *pieces, w_down, centred)
    return call(
        kernel,
        (units // step,),
        scalars,
        operands,
        [whole(o) for o in operands[:-2]]
        + [pl.BlockSpec((step, width), lambda n, _: (n, 0)), whole(centred)],
        outs,
        [pl.BlockSpec((step, rows), lambda n, _: (n, 0))] + [whole(o) for o in outs[1:]],
        [pltpu.VMEM((rows, hat_width), LOW), pltpu.VMEM((rows, cols), LOW)],
        2 * rows * width * (units + query_width),
    )


def late(feats, pooled, hid_t, centred, facts, along, back_t, hat_cols, normed_t, pre, scalars, prompt):
    rows, cols = hat_cols.shape
    units, query_width = hid_t.shape
    concepts = feats[0].shape[0]
    part = pooled.shape[1]
    wide = len(feats)
    step = min(256, units)
    model = centred.shape[0]
    groups = len(pre)
    per = rows // groups

    def kernel(scal, pool, hid, cent, facts, along, back, hat, normed, *refs):
        pre_refs, feat_refs = refs[:groups], refs[groups : groups + wide]
        up, down, proj, feat, out_grad, grad_t, act_t, weights = refs[groups + wide :]
        row = lax.broadcasted_iota(jnp.int32, (rows, concepts), 0)
        low = lax.broadcasted_iota(jnp.int32, (rows, concepts), 1) * prompt
        pick = jnp.where((row >= low) & (row < low + prompt), 1.0, 0.0).astype(LOW)

        @pl.when(pl.program_id(0) == 0)
        def _():
            total = sum(r[...].astype(FULL) for r in feat_refs)
            feat[...] = total.astype(LOW)
            proj[...] = lax.dot_general(
                pool[...].astype(FULL),
                total,
                (((0,), (0,)), ((), ())),
                precision=lax.Precision.HIGHEST,
                preferred_element_type=FULL,
            )
            known = facts[...].astype(FULL)
            inv = known[:, 0:1] + known[:, 1:2]
            lead = inv * known[:, 2:3] / known[:, 3:4]
            chosen = dot_n(pick, feat[...])
            second = jnp.sum(along[...].astype(FULL) * chosen, axis=1, keepdims=True)
            tail = lead * second * (1.0 / model)
            at = pl.multiple_of(scal[1] * cols, 128)
            grad_cols = dot_t(feat[...], cent[pl.ds(at, cols), :]).astype(LOW)
            out_grad[...] = (
                lead * dot_n(pick, grad_cols) - tail * hat[...].astype(FULL)
            ).astype(LOW)
            lane = lax.broadcasted_iota(jnp.int32, (rows, 128), 1)
            both = jnp.where(lane == 0, lead, jnp.where(lane == 1, tail, 0.0))
            weights[...] = both.T[:8]

        lead = weights[0:1, :]
        tail = weights[1:2, :]
        grad_step = dot_t(hid[...], feat[...]).astype(LOW)
        grad_rows = lead * dot_t(grad_step, pick) - tail * back[...].astype(FULL)
        for g in range(groups):
            act, slope = gelu_both(pre_refs[g][...].astype(FULL))
            span = slice(g * per, (g + 1) * per)
            act_t[:, span] = act.astype(LOW)
            grad_t[:, span] = (slope * grad_rows[:, span]).astype(LOW)
        up[...] = dot_t(normed[...], grad_t[...])
        down[...] = dot_n(act_t[...], out_grad[...])

    outs = [
        shape((cols, units), FULL),
        shape((units, cols), FULL),
        shape((part, query_width), FULL),
    ]
    operands = (
        pooled, hid_t, centred, facts, along, back_t, hat_cols, normed_t, *pre, *feats
    )
    moving = lambda wide: pl.BlockSpec((step, wide), lambda n, _: (n, 0))
    return call(
        kernel,
        (units // step,),
        scalars,
        operands,
        [
            whole(pooled),
            moving(query_width),
            whole(centred),
            whole(facts),
            whole(along),
            moving(rows),
            whole(hat_cols),
            whole(normed_t),
        ]
        + [moving(per)] * groups
        + [whole(f) for f in feats],
        outs,
        [
            pl.BlockSpec((cols, step), lambda n, _: (0, n)),
            pl.BlockSpec((step, cols), lambda n, _: (n, 0)),
            whole(outs[2]),
        ],
        [
            pltpu.VMEM((concepts, query_width), LOW),
            pltpu.VMEM((rows, cols), LOW),
            pltpu.VMEM((step, rows), LOW),
            pltpu.VMEM((step, rows), LOW),
            pltpu.VMEM((8, rows), FULL),
        ],
        4 * rows * units * cols,
    )


def body_scatter(
    prompt_embeds, prompt_len, norm_gain, w_up, w_down, final_gain, w_proj, queries, assign, valid
):
    per_group, prompt, model_width = prompt_embeds.shape
    tok_rows = per_group * prompt
    det_size = lax.axis_size("det")
    share = model_width // det_size
    offset = lax.axis_index("det") * share
    tokens = prompt_embeds.reshape(tok_rows, model_width).astype(jnp.float32)
    row_mean = jnp.mean(tokens, axis=1, keepdims=True)
    centred = tokens - row_mean
    variance = jnp.mean(centred * centred, axis=1, keepdims=True)
    normed = (centred * lax.rsqrt(variance + EPS) * norm_gain).astype(jnp.bfloat16)
    pre_act = jnp.dot(normed, w_up, preferred_element_type=jnp.float32)
    hidden_act, act_back = jax.vjp(gelu_fn, pre_act)
    hidden = hidden_act.astype(jnp.bfloat16)
    partial_out = jnp.dot(hidden, w_down, preferred_element_type=jnp.float32)
    position = lax.broadcasted_iota(jnp.int32, (per_group, prompt), 1)
    lengths = prompt_len.astype(jnp.float32)
    pool_weight = (position < prompt_len[:, None]).astype(jnp.float32) / lengths[:, None]
    layer_out = tokens + lax.psum(partial_out.astype(jnp.bfloat16), "det").astype(jnp.float32)
    out_mean = jnp.mean(layer_out, axis=1, keepdims=True)
    out_centred = layer_out - out_mean
    out_var = jnp.mean(out_centred * out_centred, axis=1, keepdims=True)
    inv_scale = lax.rsqrt(out_var + EPS)
    out_hat = out_centred * inv_scale
    final = out_hat * final_gain
    pooled_full = jnp.sum(
        final.reshape(per_group, prompt, model_width) * pool_weight[:, :, None], axis=1
    )
    pooled_share = lax.dynamic_slice_in_dim(pooled_full, offset, share, 1)
    pooled_low = pooled_share.astype(jnp.bfloat16)
    feat_part = jnp.dot(pooled_low, w_proj, preferred_element_type=jnp.float32)
    concept_feat = lax.psum(feat_part, "det").astype(jnp.bfloat16)
    all_feat = lax.all_gather(concept_feat, "text", axis=0, tiled=True)
    concept_count = all_feat.shape[0]
    img_count, query_count, query_width = queries.shape
    query_rows = img_count * query_count
    flat_queries = queries.reshape(query_rows, query_width)
    score_scale = query_width ** (-0.5)
    scores = (
        lax.dot_general(
            flat_queries, all_feat, (((1,), (1,)), ((), ())), preferred_element_type=jnp.float32
        )
        * score_scale
        + LOGIT_BIAS
    )
    column = lax.broadcasted_iota(jnp.int32, (img_count, query_count, concept_count), 2)
    target = (assign[:, :, None] == column).astype(jnp.float32).reshape(query_rows, concept_count)
    weight = jnp.broadcast_to(
        valid[:, None, :].astype(jnp.float32), (img_count, query_count, concept_count)
    ).reshape(query_rows, concept_count)
    score_grad = jax.grad(focal_total)(scores, target, weight).astype(jnp.bfloat16)
    query_grad = jnp.dot(score_grad, all_feat, preferred_element_type=jnp.float32) * score_scale
    images = img_count * lax.axis_size("text") * det_size
    feat_terms = lax.dot_general(
        score_grad, flat_queries, (((0,), (0,)), ((), ())), preferred_element_type=jnp.float32
    ) * (score_scale / images)
    feat_owned = lax.psum_scatter(
        feat_terms.astype(jnp.bfloat16), "text", scatter_dimension=0, tiled=True
    ).astype(jnp.float32)
    feat_grad = lax.psum(feat_owned, "det")
    proj_part = jnp.dot(
        pooled_low.astype(jnp.float32).T, feat_grad, precision=lax.Precision.HIGHEST
    )
    proj_grad = lax.psum(proj_part.astype(jnp.bfloat16), "text").astype(jnp.float32)
    pooled_share_grad = jnp.dot(
        feat_grad, w_proj.astype(jnp.float32).T, precision=lax.Precision.HIGHEST
    )
    pooled_whole_grad = lax.all_gather(pooled_share_grad, "det", axis=1, tiled=True)
    final_grad = (pooled_whole_grad[:, None, :] * pool_weight[:, :, None]).reshape(
        tok_rows, model_width
    )
    hat_grad = final_grad * final_gain
    mean_first = jnp.mean(hat_grad, axis=1, keepdims=True)
    mean_second = jnp.mean(hat_grad * out_hat, axis=1, keepdims=True)
    out_grad = ((hat_grad - mean_first - out_hat * mean_second) * inv_scale).astype(jnp.bfloat16)
    down_terms = lax.dot_general(
        hidden, out_grad, (((0,), (0,)), ((), ())), preferred_element_type=jnp.float32
    )
    down_grad = lax.psum_scatter(
        down_terms.astype(jnp.bfloat16), "text", scatter_dimension=1, tiled=True
    ).astype(jnp.float32)
    hidden_grad = lax.dot_general(
        out_grad, w_down, (((1,), (1,)), ((), ())), preferred_element_type=jnp.float32
    )
    pre_grad = act_back(hidden_grad)[0].astype(jnp.bfloat16)
    up_terms = lax.dot_general(
        normed, pre_grad, (((0,), (0,)), ((), ())), preferred_element_type=jnp.float32
    )
    up_grad = lax.psum_scatter(
        up_terms.astype(jnp.bfloat16), "text", scatter_dimension=0, tiled=True
    ).astype(jnp.float32)
    return (up_grad, down_grad, proj_grad, query_grad.reshape(img_count, query_count, query_width))


def body(
    prompt_embeds, prompt_len, norm_gain, w_up, w_down, final_gain, w_proj, queries, assign, valid
):
    per_group, prompt, width = prompt_embeds.shape
    tok_rows = per_group * prompt
    det_size = lax.axis_size("det")
    text_size = lax.axis_size("text")
    det = lax.axis_index("det")
    text = lax.axis_index("text")
    if 4 * text_size * tok_rows * width * 2 > ROOM or queries.shape[0] > 1:
        return body_scatter(
            prompt_embeds, prompt_len, norm_gain, w_up, w_down, final_gain, w_proj, queries,
            assign, valid
        )
    share = tok_rows // det_size
    cols = width // text_size
    part = width // det_size
    others = list(range(1, text_size))
    scalars = jnp.concatenate([jnp.stack([det, text]).astype(jnp.int32), prompt_len])
    tokens = prompt_embeds.reshape(tok_rows, width)

    cols_near, cols_far, pre_near, keep, send = front(
        tokens, norm_gain, w_up, w_down, scalars, cols, share, others
    )
    parts = scatter_parts([keep, swap(send, "det", 1)], lax.div(det, 2))
    proj_pieces, offsets = gather_pieces(w_proj)
    proj, scaled_proj, hid_t = proj_side(proj_pieces, offsets, w_down, final_gain, scalars)
    pre = [pre_near] + [swap(pre_near, "text", a) for a in others]

    packed, *packed_far = out_norm(tokens, parts, cols_far, scalars, prompt, per_group)
    near_pieces, _ = gather_pieces(packed)
    far = jnp.stack([swap(packed_far[a - 1], "text", a) for a in others])
    far_pieces, _ = gather_pieces(far)

    hat_near, feats = concept_side(
        near_pieces, offsets, proj, prompt_len[:, None], final_gain, scalars, prompt, part
    )
    feats = [feats] + [swap(feats, "text", a) for a in others]
    img_count, query_count, query_width = queries.shape

    blocks = valid.astype(FULL).reshape(text_size, per_group)
    allowed = jnp.concatenate(
        [lax.dynamic_slice_in_dim(blocks, text ^ a, 1, 0) for a in range(text_size)], 0
    ).reshape(text_size * per_group, 1)
    images = img_count * text_size * det_size
    query_grad, terms, pooled, *away = score_side(
        queries.reshape(query_count, query_width), assign, allowed, feats, scalars,
        query_width, images
    )

    total = terms.astype(FULL)
    for a in others:
        total = total + swap(away[a - 1], "text", a).astype(FULL)
    feat_parts = sum_det(total.astype(LOW))

    back_t, along, hat_cols, facts, normed_t = back_side(
        hat_near, cols_near, far_pieces, offsets, w_down, scaled_proj, scalars, cols
    )
    up_grad, down_grad, proj_grad = late(
        feat_parts, pooled, hid_t, scaled_proj, facts, along, back_t, hat_cols, normed_t, pre,
        scalars, prompt
    )
    return (up_grad, down_grad, proj_grad, query_grad.reshape(img_count, query_count, query_width))


def solution(mesh):
    return jax.shard_map(
        body,
        mesh=mesh,
        in_specs=(
            P("text", None, None),
            P("text"),
            P(),
            P(None, "det"),
            P("det", None),
            P(),
            P("det", None),
            P(("text", "det"), None, None),
            P(("text", "det"), None),
            P(("text", "det"), None),
        ),
        out_specs=(
            P("text", "det"),
            P("det", "text"),
            P("det", None),
            P(("text", "det"), None, None),
        ),
        check_vma=False,
    )
```
